512 devices in a mesh: seq: 16 (over z, core), head: 32 (over y, x).
Axes of the slice: x: 4, y: 8, z: 8, core: 2. Of those that a mesh axis runs over, the one named last changes fastest.
Arguments:
- queries: bfloat16 [65536, 4096], P(('seq', 'head')), may hold values from -6 to 6
- keys: bfloat16 [65536, 1024], P(('seq', 'head')), may hold values from -6 to 6
- values: bfloat16 [65536, 1024], P(('seq', 'head')), may hold values from -6 to 6
- out_grad: bfloat16 [65536, 4096], P(('seq', 'head')), may hold values from -6 to 6
Outputs:
- queries_grad: bfloat16 [65536, 4096], P(('seq', 'head'))
- keys_grad: bfloat16 [65536, 1024], P(('seq', 'head'))
- values_grad: bfloat16 [65536, 1024], P(('seq', 'head'))
The draws below stay inside these ranges and needn't reach their ends.
All inputs are finite; a program needn't handle non-finite values.
Results may differ from the reference program's by a relative error of at most 0.0065.
Values may be sent and summed in bfloat16 or wider, within the bound.
A program may use at most 64 MiB of HBM per device.

```python
import jax
import jax.numpy as jnp
from jax import lax

HD = 128
GROUP = 4
BLK = 256
HEADS = 32
KV_HEADS = 8
TOKENS = 65536


def levels(stream_key, dims, cuts, least, top_value):
    level, own = 1.0, jax.random.fold_in(stream_key, 6)
    for axis_at, parts in cuts:
        draws = jnp.exp(jax.random.uniform(jax.random.fold_in(own, axis_at), (parts,), jnp.float32, least / len(cuts), top_value / len(cuts)))
        level = level * jnp.repeat(draws, dims[axis_at] // parts).reshape([-1 if axis == axis_at else 1 for axis in range(len(dims))])
    return level


def bell_draw(stream_key, extent, width, reach, shards=(), kind=jnp.bfloat16):
    gain = levels(stream_key, extent, shards, -0.22, 0.18) if shards else 1.0
    entries = jax.random.normal(stream_key, extent, jnp.float32) * width * gain
    return jnp.minimum(jnp.maximum(entries, -reach), reach).astype(kind)


def setup_inputs(seed: int = 0) -> dict:
    key_of = jax.random.split(jax.random.key(seed), 5)
    return {
        "queries": bell_draw(key_of[0], (TOKENS, HEADS * HD), 1.0, 6.0, ((0, 512),)),
        "keys": bell_draw(key_of[1], (TOKENS, KV_HEADS * HD), 1.0, 6.0, ((0, 512),)),
        "values": bell_draw(key_of[2], (TOKENS, KV_HEADS * HD), 1.0, 6.0, ((0, 512),)),
        "out_grad": bell_draw(key_of[3], (TOKENS, HEADS * HD), 1.0, 6.0, ((0, 512),)),
    }


def exclusive_forward(states):
    running = jnp.cumsum(states, axis=0)
    return jnp.concatenate([jnp.zeros_like(states[:1]), running[:-1]], axis=0)

def exclusive_backward(states):
    running = jnp.cumsum(states[::-1], axis=0)[::-1]
    return jnp.concatenate([running[1:], jnp.zeros_like(states[:1])], axis=0)

def reference(queries, keys, values, out_grad):
    positions = jnp.arange(TOKENS, dtype=jnp.int32)
    scale = 1.0 / jnp.sqrt((HD * (positions + 1)).astype(jnp.float32))
    block_count = TOKENS // BLK
    causal = jnp.arange(BLK)[:, None] >= jnp.arange(BLK)[None, :]
    scale_blocks = scale.reshape(block_count, BLK)

    def one_block(pieces):
        query_block, key_block, value_block, cot_block, scaled_block, scale_block, prior_state, future_state = pieces
        key_scores = jnp.dot(query_block, key_block.T, preferred_element_type=jnp.float32)
        forward_weights = jnp.where(causal, scale_block[:, None] * key_scores, 0.0).astype(jnp.bfloat16)
        value_scores = jnp.dot(scaled_block, value_block.T, preferred_element_type=jnp.float32)
        backward_weights = jnp.where(causal, value_scores, 0.0).astype(jnp.bfloat16)
        query_grad = jnp.dot(backward_weights, key_block, preferred_element_type=jnp.float32)
        query_grad = query_grad + jnp.dot(scaled_block, prior_state.T, preferred_element_type=jnp.float32)
        key_grad = jnp.dot(backward_weights.T, query_block, preferred_element_type=jnp.float32)
        key_grad = key_grad + jnp.dot(value_block, future_state, preferred_element_type=jnp.float32)
        value_grad = jnp.dot(forward_weights.T, cot_block, preferred_element_type=jnp.float32)
        value_grad = value_grad + jnp.dot(key_block, future_state.T, preferred_element_type=jnp.float32)
        return (query_grad.astype(jnp.bfloat16), key_grad.astype(jnp.bfloat16), value_grad.astype(jnp.bfloat16))

    def head_grads(head):
        kv_index = head // GROUP
        query_cols = lax.dynamic_slice_in_dim(queries, (head * HD).astype(jnp.int32), HD, 1)
        cot_cols = lax.dynamic_slice_in_dim(out_grad, (head * HD).astype(jnp.int32), HD, 1)
        key_cols = lax.dynamic_slice_in_dim(keys, (kv_index * HD).astype(jnp.int32), HD, 1)
        value_cols = lax.dynamic_slice_in_dim(values, (kv_index * HD).astype(jnp.int32), HD, 1)
        scaled_cot = (scale[:, None] * cot_cols.astype(jnp.float32)).astype(jnp.bfloat16)
        query_blocks = query_cols.reshape(block_count, BLK, HD)
        key_blocks = key_cols.reshape(block_count, BLK, HD)
        value_blocks = value_cols.reshape(block_count, BLK, HD)
        cot_blocks = cot_cols.reshape(block_count, BLK, HD)
        scaled_blocks = scaled_cot.reshape(block_count, BLK, HD)
        pair_states = jnp.einsum('bsd,bse->bde', key_blocks.astype(jnp.float32), value_blocks.astype(jnp.float32), precision=lax.Precision.HIGHEST)
        grad_states = jnp.einsum('bte,btd->bed', scaled_blocks.astype(jnp.float32), query_blocks.astype(jnp.float32), precision=lax.Precision.HIGHEST)
        prior_states = exclusive_forward(pair_states).astype(jnp.bfloat16)
        future_states = exclusive_backward(grad_states).astype(jnp.bfloat16)
        return lax.map(one_block, (query_blocks, key_blocks, value_blocks, cot_blocks, scaled_blocks, scale_blocks, prior_states, future_states))
    query_grad, key_grad, value_grad = lax.map(head_grads, jnp.arange(HEADS, dtype=jnp.int32))
    queries_grad = query_grad.reshape(HEADS, TOKENS, HD).transpose(1, 0, 2).reshape(TOKENS, HEADS * HD)
    key_sum = lax.optimization_barrier(jnp.sum(key_grad.reshape(KV_HEADS, GROUP, TOKENS, HD).astype(jnp.float32), axis=1)).astype(jnp.bfloat16)
    value_sum = lax.optimization_barrier(jnp.sum(value_grad.reshape(KV_HEADS, GROUP, TOKENS, HD).astype(jnp.float32), axis=1)).astype(jnp.bfloat16)
    keys_grad = key_sum.transpose(1, 0, 2).reshape(TOKENS, KV_HEADS * HD)
    values_grad = value_sum.transpose(1, 0, 2).reshape(TOKENS, KV_HEADS * HD)
    return (queries_grad, keys_grad, values_grad)
```

```python
import functools

import jax
import jax.numpy as jnp
from jax import lax
from jax.experimental import pallas as pl
from jax.experimental.pallas import tpu as pltpu
from jax.sharding import PartitionSpec as P

HD = 128
GROUP = 4
KV = 8
RING_X = 4
SUB = 2
MESH = pl.DeviceIdType.MESH
F32 = jnp.float32
BF16 = jnp.bfloat16


def dot(left, right, left_dim, right_dim):
    return lax.dot_general(
        left, right, (((left_dim,), (right_dim,)), ((), ())), preferred_element_type=F32
    )


def kernel(
    nx, ny, nw,
    q_hbm, k_hbm, v_hbm, o_hbm, dq, dk, dv,
    q, k, v, o, s, dq_sum, dk_sum, dv_sum,
    x_out, x_in, y_out, y_in, z_out, z_in, yb_out, yb_in, xb_out, state,
    load_sem, send_sem, recv_sem, z_send, z_recv,
):
    w = lax.axis_index("seq")
    head = lax.axis_index("head")
    y, x = head // nx, head % nx
    mats = KV // nx // SUB
    rows = HD // ny
    tokens = q_hbm.shape[0]

    barrier = pltpu.get_barrier_semaphore()

    def greet(seq_to, head_to):
        pl.semaphore_signal(barrier, inc=1, device_id=(seq_to, head_to), device_id_type=MESH)

    for d in range(1, nx):
        greet(w, y * nx + (x + d) % nx)
    for d in range(1, ny):
        greet(w, (y + d) % ny * nx + x)

    @pl.loop(1, nw)
    def _(d):
        greet((w + d) % nw, head)

    loads = [
        pltpu.make_async_copy(src, dst, load_sem.at[i])
        for i, (src, dst) in enumerate(((k_hbm, k), (v_hbm, v), (o_hbm, o), (q_hbm, q)))
    ]
    for load in loads:
        load.start()

    first = (w * nx * ny + head) * tokens + 1

    def scale_along(axis):
        place = first + lax.broadcasted_iota(jnp.int32, (tokens, HD), axis)
        return 1.0 / jnp.sqrt((HD * place).astype(F32))

    def chunk(kind, sub):
        return kind * SUB + sub

    def remote(src, dst, stage, c, seq_to, head_to):
        return pltpu.make_async_remote_copy(
            src_ref=src, dst_ref=dst, send_sem=send_sem.at[stage, c], recv_sem=recv_sem.at[stage, c],
            device_id=(seq_to, head_to), device_id_type=MESH,
        )

    def all_x(src, dst, stage, kind, sub):
        return remote(
            src.at[kind, sub, pl.ds(0, nx - 1)], dst.at[kind, sub, pl.ds(0, nx - 1)],
            stage, chunk(kind, sub), w, y * nx + (x + 1) % nx,
        )

    def all_y(src, dst, stage, kind, sub):
        return remote(
            src.at[kind, sub, pl.ds(0, ny - 1)], dst.at[kind, sub, pl.ds(0, ny - 1)],
            stage, chunk(kind, sub), w, (y + 1) % ny * nx + x,
        )

    def send_x(src, dst, stage, kind, sub):
        for d in range(1, nx):
            to = (x + d) % nx
            remote(
                src.at[kind, sub, to], dst.at[kind, sub, x], stage, chunk(kind, sub), w, y * nx + to
            ).start()
        dst[kind, sub, x] = src[kind, sub, x]

    def send_y(src, dst, stage, kind, sub):
        for d in range(1, ny):
            to = (y + d) % ny
            remote(
                src.at[kind, sub, to], dst.at[kind, sub, y], stage, chunk(kind, sub), w, to * nx + x
            ).start()
        dst[kind, sub, y] = src[kind, sub, y]

    def z_copy(kind, sub, to, origin):
        return pltpu.make_async_remote_copy(
            src_ref=z_out.at[kind, sub], dst_ref=z_in.at[kind, sub, origin],
            send_sem=z_send.at[sub, to], recv_sem=z_recv.at[sub, origin],
            device_id=(to, head), device_id_type=MESH,
        )

    def order(kind, count):
        return range(count) if kind == 0 else range(count - 1, -1, -1)

    def after_x(kind, sub):
        all_x(x_out, x_in, 0, kind, sub).wait_recv()
        total = x_in[kind, sub, 0].astype(F32)
        for i in range(1, nx):
            total = total + x_in[kind, sub, i].astype(F32)
        total = total.astype(BF16)
        for i in range(ny):
            y_out[kind, sub, i] = total[:, i * rows : (i + 1) * rows]
        send_y(y_out, y_in, 1, kind, sub)

    def after_y(kind, sub):
        all_y(y_out, y_in, 1, kind, sub).wait_recv()
        total = y_in[kind, sub, 0].astype(F32)
        for i in range(1, ny):
            total = total + y_in[kind, sub, i].astype(F32)
        z_out[kind, sub] = total.astype(BF16)
        low, high = (w + 1, nw) if kind == 0 else (0, w)

        @pl.loop(low, high)
        def _(to):
            z_copy(kind, sub, to, w).start()

    def after_z(kind, sub):
        low, high = (0, w) if kind == 0 else (w + 1, nw)

        @pl.loop(low, high)
        def _(origin):
            z_copy(kind, sub, origin, origin).wait_recv()

        def add(origin, total):
            return total + z_in[kind, sub, origin].astype(F32)

        running = lax.fori_loop(low, high, add, jnp.zeros((mats, rows, HD), F32))
        for i in order(kind, ny):
            yb_out[kind, sub, i] = running.astype(BF16)
            running = running + y_in[kind, sub, i].astype(F32)
        send_y(yb_out, yb_in, 2, kind, sub)

    def after_yb(kind, sub):
        all_y(yb_out, yb_in, 2, kind, sub).wait_recv()
        for i in range(ny):
            part = slice(i * rows, (i + 1) * rows)
            running = yb_in[kind, sub, i].astype(F32)
            for j in order(kind, nx):
                xb_out[kind, sub, j, :, part] = running.astype(BF16)
                running = running + x_in[kind, sub, j, :, part].astype(F32)
        send_x(xb_out, state, 3, kind, sub)

    def cols(index, count=1):
        return pl.ds(pl.multiple_of(index * HD, HD), count * HD)

    def each_group(step):
        @pl.loop(0, nx)
        def _(owner):
            for sub in range(SUB):
                for m in range(mats):
                    step(owner * (KV // nx) + sub * mats + m, owner, sub, m)

    loads[0].wait()
    loads[1].wait()

    def pair_state(g, owner, sub, m):
        x_out[0, sub, owner, m] = dot(k[:, cols(g)], v[:, cols(g)], 0, 0).astype(BF16)

    each_group(pair_state)
    pl.semaphore_wait(barrier, nx - 1 + ny - 1 + nw - 1)
    for sub in range(SUB):
        send_x(x_out, x_in, 0, 0, sub)

    scale_rows = scale_along(0)
    loads[2].wait()
    loads[3].wait()

    def stacked(ref, g):
        return jnp.concatenate([ref[:, cols(g * GROUP + i)] for i in range(GROUP)], axis=0)

    def grad_state(g, owner, sub, m):
        for i in range(GROUP):
            at = cols(g * GROUP + i)
            s[:, at] = (scale_rows * o[:, at].astype(F32)).astype(BF16)
        x_out[1, sub, owner, m] = dot(stacked(s, g), stacked(q, g), 0, 0).astype(BF16)

    each_group(grad_state)
    for sub in range(SUB):
        send_x(x_out, x_in, 0, 1, sub)
    for sub in range(SUB):
        after_x(0, sub)

    scale_cols = scale_along(1)
    row = lax.broadcasted_iota(jnp.int32, (tokens, tokens), 0)
    col = lax.broadcasted_iota(jnp.int32, (tokens, tokens), 1)

    def within(low, high):
        @pl.loop(low, high)
        def _(g):
            key, value = k[:, cols(g)], v[:, cols(g)]
            forward, backward = [], []
            for i in range(GROUP):
                at = cols(g * GROUP + i)
                weights = scale_cols * dot(key, q[:, at], 1, 1)
                forward.append(jnp.where(row <= col, weights, 0.0).astype(BF16))
                weights = dot(value, s[:, at], 1, 1)
                backward.append(jnp.where(row <= col, weights, 0.0).astype(BF16))
                weights = dot(s[:, at], value, 1, 1)
                weights = jnp.where(col <= row, weights, 0.0).astype(BF16)
                dq_sum[:, at] = dot(weights, key, 1, 0)
            dk_sum[:, cols(g)] = dot(jnp.concatenate(backward, axis=1), stacked(q, g), 1, 0)
            dv_sum[:, cols(g)] = dot(jnp.concatenate(forward, axis=1), stacked(o, g), 1, 0)

    within(0, 2)
    for sub in range(SUB):
        after_x(1, sub)
    for sub in range(SUB):
        after_y(0, sub)
    within(2, 4)
    for sub in range(SUB):
        after_y(1, sub)
    for sub in range(SUB):
        after_z(0, sub)
    within(4, 6)
    for sub in range(SUB):
        after_z(1, sub)
    for sub in range(SUB):
        after_yb(0, sub)
    within(6, 8)
    for sub in range(SUB):
        after_yb(1, sub)

    for sub in range(SUB):
        all_x(xb_out, state, 3, 0, sub).wait_recv()

    def finish_query(g, owner, sub, m):
        add = dot(stacked(s, g), state[0, sub, owner, m], 1, 1)
        for i in range(GROUP):
            at = cols(g * GROUP + i)
            dq[:, at] = (dq_sum[:, at] + add[i * tokens : (i + 1) * tokens]).astype(BF16)

    each_group(finish_query)
    for sub in range(SUB):
        all_x(xb_out, state, 3, 1, sub).wait_recv()

    def finish_pair(g, owner, sub, m):
        future = state[1, sub, owner, m]
        at = cols(g)
        dk[:, at] = (dk_sum[:, at] + dot(v[:, at], future, 1, 0)).astype(BF16)
        dv[:, at] = (dv_sum[:, at] + dot(k[:, at], future, 1, 1)).astype(BF16)

    each_group(finish_pair)

    for kind in range(2):
        for sub in range(SUB):
            all_x(x_out, x_in, 0, kind, sub).wait_send()
            all_y(y_out, y_in, 1, kind, sub).wait_send()
            all_y(yb_out, yb_in, 2, kind, sub).wait_send()
            all_x(xb_out, state, 3, kind, sub).wait_send()
            low, high = (w + 1, nw) if kind == 0 else (0, w)

            @pl.loop(low, high)
            def _(to):
                z_copy(kind, sub, to, w).wait_send()


def body(nx, ny, nw, queries, keys, values, out_grad):
    tokens = queries.shape[0]
    mats = KV // nx // SUB
    rows = HD // ny
    wide, narrow = (tokens, queries.shape[1]), (tokens, keys.shape[1])
    by_x = pltpu.VMEM((2, SUB, nx, mats, HD, HD), BF16)
    by_y = pltpu.VMEM((2, SUB, ny, mats, rows, HD), BF16)
    return pl.pallas_call(
        functools.partial(kernel, nx, ny, nw),
        out_shape=(
            pltpu.VMEM(wide, BF16),
            pltpu.VMEM(narrow, BF16),
            pltpu.VMEM(narrow, BF16),
        ),
        in_specs=[pl.BlockSpec(memory_space=pltpu.HBM)] * 4,
        out_specs=(pl.BlockSpec(memory_space=pltpu.VMEM),) * 3,
        scratch_shapes=[
            pltpu.VMEM(wide, BF16),
            pltpu.VMEM(narrow, BF16),
            pltpu.VMEM(narrow, BF16),
            pltpu.VMEM(wide, BF16),
            pltpu.VMEM(wide, BF16),
            pltpu.VMEM(wide, F32),
            pltpu.VMEM(narrow, F32),
            pltpu.VMEM(narrow, F32),
            by_x,
            by_x,
            by_y,
            by_y,
            pltpu.VMEM((2, SUB, mats, rows, HD), BF16),
            pltpu.VMEM((2, SUB, nw, mats, rows, HD), BF16),
            by_y,
            by_y,
            by_x,
            by_x,
            pltpu.SemaphoreType.DMA((4,)),
            pltpu.SemaphoreType.DMA((4, 2 * SUB)),
            pltpu.SemaphoreType.DMA((4, 2 * SUB)),
            pltpu.SemaphoreType.DMA((SUB, nw)),
            pltpu.SemaphoreType.DMA((SUB, nw)),
        ],
        compiler_params=pltpu.CompilerParams(
            collective_id=0, has_side_effects=True, vmem_limit_bytes=48 * 2**20
        ),
    )(*(pltpu.with_memory_space_constraint(a, pltpu.HBM) for a in (queries, keys, values, out_grad)))


def solution(mesh, nx=RING_X):
    nw, heads = mesh.shape["seq"], mesh.shape["head"]
    spec = P(("seq", "head"), None)
    return jax.shard_map(
        functools.partial(body, nx, heads // nx, nw),
        mesh=mesh,
        in_specs=(spec,) * 4,
        out_specs=(spec,) * 3,
        check_vma=False,
    )
```

```python
import functools

import jax
import jax.numpy as jnp
from jax import lax
from jax.experimental import pallas as pl
from jax.experimental.pallas import tpu as pltpu
from jax.sharding import PartitionSpec as P

HD = 128
GROUP = 4
KV = 8
RING_X = 4
SUB = 2
MESH = pl.DeviceIdType.MESH
F32 = jnp.float32
BF16 = jnp.bfloat16


def far_first(count):
    return sorted(range(1, count), key=lambda d: -min(d, count - d))


def dot(left, right, left_dim, right_dim):
    return lax.dot_general(
        left, right, (((left_dim,), (right_dim,)), ((), ())), preferred_element_type=F32
    )


def kernel(
    nx, ny, nw,
    q_hbm, k_hbm, v_hbm, o_hbm, dq, dk, dv,
    q, k, v, o, s, dq_sum, dk_sum, dv_sum,
    x_out, x_in, y_out, y_in, z_out, z_in, yb_out, yb_in, xb_out, state,
    load_sem, send_sem, recv_sem, z_send, z_recv, here,
):
    w = lax.axis_index("seq")
    head = lax.axis_index("head")
    y, x = head // nx, head % nx
    mats = KV // nx // SUB
    rows = HD // ny
    tokens = q_hbm.shape[0]

    barrier = pltpu.get_barrier_semaphore()

    def greet(seq_to, head_to):
        pl.semaphore_signal(barrier, inc=1, device_id=(seq_to, head_to), device_id_type=MESH)

    for d in far_first(nx):
        greet(w, y * nx + (x + d) % nx)

    def rank_of(place):
        far = 2 * place // (ny + 1)
        return (1 - far) * (2 * place - 1) + far * 2 * (ny - place) + (ny - place) // ny

    rank = rank_of(y)

    def each_column(step, above):
        for d in far_first(ny):
            other = (y + d) % ny

            @pl.when(rank_of(other) > rank if above else rank_of(other) < rank)
            def _():
                step(w, other * nx + x)

    each_column(greet, True)

    @pl.loop(w + 1, nw)
    def _(later_seq):
        greet(later_seq, head)

    loads = [
        pltpu.make_async_copy(src, dst, load_sem.at[i])
        for i, (src, dst) in enumerate(((o_hbm, o), (q_hbm, q), (k_hbm, k), (v_hbm, v)))
    ]
    for load in loads:
        load.start()

    first = (w * nx * ny + head) * tokens + 1

    def scale_along(axis):
        place = first + lax.broadcasted_iota(jnp.int32, (tokens, HD), axis)
        return 1.0 / jnp.sqrt((HD * place).astype(F32))

    def chunk(kind, sub):
        return kind * SUB + sub

    def remote(src, dst, stage, c, seq_to, head_to):
        return pltpu.make_async_remote_copy(
            src_ref=src, dst_ref=dst, send_sem=send_sem.at[stage, c], recv_sem=recv_sem.at[stage, c],
            device_id=(seq_to, head_to), device_id_type=MESH,
        )

    def all_x(src, dst, stage, kind, sub):
        return remote(
            src.at[kind, sub, pl.ds(0, nx - 1)], dst.at[kind, sub, pl.ds(0, nx - 1)],
            stage, chunk(kind, sub), w, y * nx + (x + 1) % nx,
        )

    def all_y(src, dst, stage, kind, sub):
        return remote(
            src.at[kind, sub, pl.ds(0, ny - 1)], dst.at[kind, sub, pl.ds(0, ny - 1)],
            stage, chunk(kind, sub), w, (y + 1) % ny * nx + x,
        )

    def send_x(src, dst, stage, kind, sub):
        for d in far_first(nx):
            to = (x + d) % nx
            remote(
                src.at[kind, sub, to], dst.at[kind, sub, x], stage, chunk(kind, sub), w, y * nx + to
            ).start()
        dst[kind, sub, x] = src[kind, sub, x]

    def send_y(src, dst, stage, kind, sub):
        for d in far_first(ny):
            to = (y + d) % ny
            remote(
                src.at[kind, sub, to], dst.at[kind, sub, y], stage, chunk(kind, sub), w, to * nx + x
            ).start()
        dst[kind, sub, y] = src[kind, sub, y]

    def z_copy(kind, sub, to, origin):
        return pltpu.make_async_remote_copy(
            src_ref=z_out.at[kind, sub], dst_ref=z_in.at[kind, sub, origin],
            send_sem=z_send.at[sub, to], recv_sem=z_recv.at[sub, origin],
            device_id=(to, head), device_id_type=MESH,
        )

    def order(kind, count):
        return range(count) if kind == 0 else range(count - 1, -1, -1)

    def after_x(kind, sub):
        all_x(x_out, x_in, 0, kind, sub).wait_recv()
        total = x_in[kind, sub, 0].astype(F32)
        for i in range(1, nx):
            total = total + x_in[kind, sub, i].astype(F32)
        total = total.astype(BF16)
        for i in range(ny):
            y_out[kind, sub, i] = total[:, i * rows : (i + 1) * rows]
        send_y(y_out, y_in, 1, kind, sub)

    def after_y(kind, sub):
        all_y(y_out, y_in, 1, kind, sub).wait_recv()
        total = y_in[kind, sub, 0].astype(F32)
        for i in range(1, ny):
            total = total + y_in[kind, sub, i].astype(F32)
        z_out[kind, sub] = total.astype(BF16)
        low, high = (w + 1, nw) if kind == 0 else (0, w)

        @pl.loop(low, high)
        def _(to):
            z_copy(kind, sub, to, w).start()

    def after_z(kind, sub):
        low, high = (0, w) if kind == 0 else (w + 1, nw)

        def add(origin, total):
            z_copy(kind, sub, origin, origin).wait_recv()
            return total + z_in[kind, sub, origin].astype(F32)

        running = lax.fori_loop(low, high, add, jnp.zeros((mats, rows, HD), F32))
        for i in order(kind, ny):
            yb_out[kind, sub, i] = running.astype(BF16)
            running = running + y_in[kind, sub, i].astype(F32)
        send_y(yb_out, yb_in, 2, kind, sub)

    def after_yb(kind, sub):
        all_y(yb_out, yb_in, 2, kind, sub).wait_recv()
        for i in range(ny):
            part = slice(i * rows, (i + 1) * rows)
            running = yb_in[kind, sub, i].astype(F32)
            for j in order(kind, nx):
                xb_out[kind, sub, j, :, part] = running.astype(BF16)
                running = running + x_in[kind, sub, j, :, part].astype(F32)
        send_x(xb_out, state, 3, kind, sub)

    def cols(index):
        return slice(index * HD, (index + 1) * HD)

    def each_group(step, subs=range(SUB)):
        for sub in subs:
            for owner in range(nx):
                for m in range(mats):
                    step(owner * (KV // nx) + sub * mats + m, owner, sub, m)

    def stacked(ref, g):
        return jnp.concatenate([ref[:, cols(g * GROUP + i)] for i in range(GROUP)], axis=0)

    scale_rows = scale_along(0)
    loads[0].wait()
    loads[1].wait()

    def grad_state(g, owner, sub, m):
        total = jnp.zeros((HD, HD), F32)
        for i in range(GROUP):
            at = cols(g * GROUP + i)
            scaled = (scale_rows * o[:, at].astype(F32)).astype(BF16)
            s[:, at] = scaled
            total = total + dot(scaled, q[:, at], 0, 0)
        x_out[1, sub, owner, m] = total.astype(BF16)

    each_group(grad_state)
    pl.semaphore_wait(barrier, nx - 1 + rank + w)
    for sub in range(SUB):
        send_x(x_out, x_in, 0, 1, sub)

    def answer(seq_to, head_to, sem):
        pl.semaphore_signal(sem, inc=1, device_id=(seq_to, head_to), device_id_type=MESH)

    each_column(functools.partial(answer, sem=here.at[0]), False)

    @pl.loop(0, w)
    def _(earlier_seq):
        answer(earlier_seq, head, here.at[1])

    def await_answers(sem, count):
        @pl.when(count > 0)
        def _():
            pl.semaphore_wait(sem, count)

    loads[2].wait()
    loads[3].wait()

    def pair_state(g, owner, sub, m):
        x_out[0, sub, owner, m] = dot(k[:, cols(g)], v[:, cols(g)], 0, 0).astype(BF16)

    each_group(pair_state)
    for sub in range(SUB):
        send_x(x_out, x_in, 0, 0, sub)

    scale_cols = jnp.concatenate([scale_along(1)] * GROUP, axis=1)
    row = lax.broadcasted_iota(jnp.int32, (tokens, tokens), 0)
    col = lax.broadcasted_iota(jnp.int32, (tokens, tokens), 1)
    later = jnp.concatenate([row <= col] * GROUP, axis=1)
    earlier = jnp.concatenate([col <= row] * GROUP, axis=0)

    def within(g):
        key, value = k[:, cols(g)], v[:, cols(g)]
        query, scaled, cot = stacked(q, g), stacked(s, g), stacked(o, g)
        forward = jnp.where(later, scale_cols * dot(key, query, 1, 1), 0.0).astype(BF16)
        backward = jnp.where(later, dot(value, scaled, 1, 1), 0.0).astype(BF16)
        weights = jnp.where(earlier, dot(scaled, value, 1, 1), 0.0).astype(BF16)
        part = dot(weights, key, 1, 0)
        for i in range(GROUP):
            dq_sum[:, cols(g * GROUP + i)] = part[i * tokens : (i + 1) * tokens]
        dk_sum[:, cols(g)] = dot(backward, query, 1, 0)
        dv_sum[:, cols(g)] = dot(forward, cot, 1, 0)

    for g in range(KV):
        within(g)
    def each_sub(step, kind):
        for sub in range(SUB):
            step(kind, sub)

    await_answers(here.at[0], ny - 1 - rank)
    each_sub(after_x, 1)
    each_sub(after_x, 0)
    each_sub(after_y, 1)
    await_answers(here.at[1], nw - 1 - w)
    each_sub(after_y, 0)
    each_sub(after_z, 0)
    each_sub(after_yb, 0)
    each_sub(after_z, 1)

    def finish_query(g, owner, sub, m):
        add = dot(stacked(s, g), state[0, sub, owner, m], 1, 1)
        for i in range(GROUP):
            at = cols(g * GROUP + i)
            dq[:, at] = (dq_sum[:, at] + add[i * tokens : (i + 1) * tokens]).astype(BF16)

    def finish_pair(g, owner, sub, m):
        future = state[1, sub, owner, m]
        at = cols(g)
        dk[:, at] = (dk_sum[:, at] + dot(v[:, at], future, 1, 0)).astype(BF16)
        dv[:, at] = (dv_sum[:, at] + dot(k[:, at], future, 1, 1)).astype(BF16)

    def finish(kind, step):
        for sub in range(SUB):
            all_x(xb_out, state, 3, kind, sub).wait_recv()
            each_group(step, (sub,))

    finish(0, finish_query)
    each_sub(after_yb, 1)
    finish(1, finish_pair)

    for kind in range(2):
        for sub in range(SUB):
            all_x(x_out, x_in, 0, kind, sub).wait_send()
            all_y(y_out, y_in, 1, kind, sub).wait_send()
            all_y(yb_out, yb_in, 2, kind, sub).wait_send()
            all_x(xb_out, state, 3, kind, sub).wait_send()
            low, high = (w + 1, nw) if kind == 0 else (0, w)

            @pl.loop(low, high)
            def _(to):
                z_copy(kind, sub, to, w).wait_send()


def write_back(*refs):
    sources, results, sems = refs[:3], refs[3:6], refs[6]
    copies = [
        pltpu.make_async_copy(source, result, sems.at[i])
        for i, (source, result) in enumerate(zip(sources, results))
    ]
    for copy in copies:
        copy.start()
    for copy in copies:
        copy.wait()


def body(nx, ny, nw, queries, keys, values, out_grad):
    tokens = queries.shape[0]
    mats = KV // nx // SUB
    rows = HD // ny
    wide, narrow = (tokens, queries.shape[1]), (tokens, keys.shape[1])
    by_x = pltpu.VMEM((2, SUB, nx, mats, HD, HD), BF16)
    by_y = pltpu.VMEM((2, SUB, ny, mats, rows, HD), BF16)
    grads = pl.pallas_call(
        functools.partial(kernel, nx, ny, nw),
        out_shape=(
            pltpu.VMEM(wide, BF16),
            pltpu.VMEM(narrow, BF16),
            pltpu.VMEM(narrow, BF16),
        ),
        in_specs=[pl.BlockSpec(memory_space=pltpu.HBM)] * 4,
        out_specs=(pl.BlockSpec(memory_space=pltpu.VMEM),) * 3,
        scratch_shapes=[
            pltpu.VMEM(wide, BF16),
            pltpu.VMEM(narrow, BF16),
            pltpu.VMEM(narrow, BF16),
            pltpu.VMEM(wide, BF16),
            pltpu.VMEM(wide, BF16),
            pltpu.VMEM(wide, F32),
            pltpu.VMEM(narrow, F32),
            pltpu.VMEM(narrow, F32),
            by_x,
            by_x,
            by_y,
            by_y,
            pltpu.VMEM((2, SUB, mats, rows, HD), BF16),
            pltpu.VMEM((2, SUB, nw, mats, rows, HD), BF16),
            by_y,
            by_y,
            by_x,
            by_x,
            pltpu.SemaphoreType.DMA((4,)),
            pltpu.SemaphoreType.DMA((4, 2 * SUB)),
            pltpu.SemaphoreType.DMA((4, 2 * SUB)),
            pltpu.SemaphoreType.DMA((SUB, nw)),
            pltpu.SemaphoreType.DMA((SUB, nw)),
            pltpu.SemaphoreType.REGULAR((2,)),
        ],
        compiler_params=pltpu.CompilerParams(
            collective_id=0, has_side_effects=True, vmem_limit_bytes=48 * 2**20
        ),
    )(*(pltpu.with_memory_space_constraint(a, pltpu.HBM) for a in (queries, keys, values, out_grad)))
    return pl.pallas_call(
        write_back,
        out_shape=(pltpu.HBM(wide, BF16), pltpu.HBM(narrow, BF16), pltpu.HBM(narrow, BF16)),
        in_specs=[pl.BlockSpec(memory_space=pltpu.VMEM)] * 3,
        out_specs=(pl.BlockSpec(memory_space=pltpu.HBM),) * 3,
        scratch_shapes=[pltpu.SemaphoreType.DMA((3,))],
        compiler_params=pltpu.CompilerParams(vmem_limit_bytes=16 * 2**20),
    )(*grads)


def solution(mesh, nx=RING_X):
    nw, heads = mesh.shape["seq"], mesh.shape["head"]
    spec = P(("seq", "head"), None)
    return jax.shard_map(
        functools.partial(body, nx, heads // nx, nw),
        mesh=mesh,
        in_specs=(spec,) * 4,
        out_specs=(spec,) * 3,
        check_vma=False,
    )
```

```python
import functools

import jax
import jax.numpy as jnp
from jax import lax
from jax.experimental import pallas as pl
from jax.experimental.pallas import tpu as pltpu
from jax.sharding import PartitionSpec as P

HD = 128
GROUP = 4
KV = 8
RING_X = 4
SUB = 2
MESH = pl.DeviceIdType.MESH
F32 = jnp.float32
BF16 = jnp.bfloat16


def far_first(count):
    return sorted(range(1, count), key=lambda d: -min(d, count - d))


def dot(left, right, left_dim, right_dim):
    return lax.dot_general(
        left, right, (((left_dim,), (right_dim,)), ((), ())), preferred_element_type=F32
    )


def kernel(
    nx, ny, nw,
    q_hbm, k_hbm, v_hbm, o_hbm, dq, dk, dv,
    q, k, v, o, s, dq_sum, dk_sum, dv_sum,
    x_out, x_in, y_out, y_in, z_out, z_in, yb_out, yb_in, xb_out, state,
    load_sem, send_sem, recv_sem, z_send, z_recv, here,
):
    w = lax.axis_index("seq")
    head = lax.axis_index("head")
    y, x = head // nx, head % nx
    mats = KV // nx // SUB
    rows = HD // ny
    tokens = q_hbm.shape[0]

    barrier = pltpu.get_barrier_semaphore()

    def greet(seq_to, head_to):
        pl.semaphore_signal(barrier, inc=1, device_id=(seq_to, head_to), device_id_type=MESH)

    for d in far_first(nx):
        greet(w, y * nx + (x + d) % nx)

    def rank_of(place):
        far = 2 * place // (ny + 1)
        return (1 - far) * (2 * place - 1) + far * 2 * (ny - place) + (ny - place) // ny

    rank = rank_of(y)

    def each_column(step, above):
        for d in far_first(ny):
            other = (y + d) % ny

            @pl.when(rank_of(other) > rank if above else rank_of(other) < rank)
            def _():
                step(w, other * nx + x)

    each_column(greet, True)

    @pl.loop(w + 1, nw)
    def _(later_seq):
        greet(later_seq, head)

    def half(sub):
        return pl.ds(sub * (q.shape[1] // SUB), q.shape[1] // SUB)

    loads = [
        pltpu.make_async_copy(src, dst, load_sem.at[i])
        for i, (src, dst) in enumerate(
            [
                (ref_from.at[:, half(sub)], ref_to.at[:, half(sub)])
                for sub in range(SUB)
                for ref_from, ref_to in ((o_hbm, o), (q_hbm, q))
            ]
            + [(k_hbm, k), (v_hbm, v)]
        )
    ]
    for load in loads:
        load.start()

    first = (w * nx * ny + head) * tokens + 1

    def scale_along(axis):
        place = first + lax.broadcasted_iota(jnp.int32, (tokens, HD), axis)
        return 1.0 / jnp.sqrt((HD * place).astype(F32))

    def chunk(kind, sub):
        return kind * SUB + sub

    def remote(src, dst, stage, c, seq_to, head_to):
        return pltpu.make_async_remote_copy(
            src_ref=src, dst_ref=dst, send_sem=send_sem.at[stage, c], recv_sem=recv_sem.at[stage, c],
            device_id=(seq_to, head_to), device_id_type=MESH,
        )

    def all_x(src, dst, stage, kind, sub):
        return remote(
            src.at[kind, sub, pl.ds(0, nx - 1)], dst.at[kind, sub, pl.ds(0, nx - 1)],
            stage, chunk(kind, sub), w, y * nx + (x + 1) % nx,
        )

    def all_y(src, dst, stage, kind, sub):
        return remote(
            src.at[kind, sub, pl.ds(0, ny - 1)], dst.at[kind, sub, pl.ds(0, ny - 1)],
            stage, chunk(kind, sub), w, (y + 1) % ny * nx + x,
        )

    def send_x(src, dst, stage, kind, sub):
        for d in far_first(nx):
            to = (x + d) % nx
            remote(
                src.at[kind, sub, to], dst.at[kind, sub, x], stage, chunk(kind, sub), w, y * nx + to
            ).start()
        dst[kind, sub, x] = src[kind, sub, x]

    def send_y(src, dst, stage, kind, sub):
        for d in far_first(ny):
            to = (y + d) % ny
            remote(
                src.at[kind, sub, to], dst.at[kind, sub, y], stage, chunk(kind, sub), w, to * nx + x
            ).start()
        dst[kind, sub, y] = src[kind, sub, y]

    def z_copy(kind, sub, to, origin):
        return pltpu.make_async_remote_copy(
            src_ref=z_out.at[kind, sub], dst_ref=z_in.at[kind, sub, origin],
            send_sem=z_send.at[sub, to], recv_sem=z_recv.at[sub, origin],
            device_id=(to, head), device_id_type=MESH,
        )

    def order(kind, count):
        return range(count) if kind == 0 else range(count - 1, -1, -1)

    def after_x(kind, sub):
        all_x(x_out, x_in, 0, kind, sub).wait_recv()
        total = x_in[kind, sub, 0].astype(F32)
        for i in range(1, nx):
            total = total + x_in[kind, sub, i].astype(F32)
        total = total.astype(BF16)
        for i in range(ny):
            y_out[kind, sub, i] = total[:, i * rows : (i + 1) * rows]
        send_y(y_out, y_in, 1, kind, sub)

    def after_y(kind, sub, end=nw):
        all_y(y_out, y_in, 1, kind, sub).wait_recv()
        total = y_in[kind, sub, 0].astype(F32)
        for i in range(1, ny):
            total = total + y_in[kind, sub, i].astype(F32)
        z_out[kind, sub] = total.astype(BF16)
        start_z(kind, sub, *((w + 1, end) if kind == 0 else (0, w)))

    def start_z(kind, sub, low, high):
        @pl.loop(low, high)
        def _(to):
            z_copy(kind, sub, to, w).start()

    def after_z(kind, sub):
        low, high = (0, w) if kind == 0 else (w + 1, nw)

        def add(origin, total):
            z_copy(kind, sub, origin, origin).wait_recv()
            return total + z_in[kind, sub, origin].astype(F32)

        running = lax.fori_loop(low, high, add, jnp.zeros((mats, rows, HD), F32))
        for i in order(kind, ny):
            yb_out[kind, sub, i] = running.astype(BF16)
            running = running + y_in[kind, sub, i].astype(F32)
        send_y(yb_out, yb_in, 2, kind, sub)

    def after_yb(kind, sub):
        all_y(yb_out, yb_in, 2, kind, sub).wait_recv()
        for i in range(ny):
            part = slice(i * rows, (i + 1) * rows)
            running = yb_in[kind, sub, i].astype(F32)
            for j in order(kind, nx):
                xb_out[kind, sub, j, :, part] = running.astype(BF16)
                running = running + x_in[kind, sub, j, :, part].astype(F32)
        send_x(xb_out, state, 3, kind, sub)

    def cols(index):
        return slice(index * HD, (index + 1) * HD)

    def each_group(step, subs=range(SUB)):
        for sub in subs:
            for owner in range(nx):
                for m in range(mats):
                    step(sub * (KV // SUB) + owner * mats + m, owner, sub, m)

    def stacked(ref, g):
        return jnp.concatenate([ref[:, cols(g * GROUP + i)] for i in range(GROUP)], axis=0)

    pl.semaphore_wait(barrier, nx - 1 + rank + w)

    def answer(seq_to, head_to, sem):
        pl.semaphore_signal(sem, inc=1, device_id=(seq_to, head_to), device_id_type=MESH)

    each_column(functools.partial(answer, sem=here.at[0]), False)

    @pl.loop(0, w)
    def _(earlier_seq):
        answer(earlier_seq, head, here.at[1 + w // (nw // 2)])

    early = w < nw // 2

    scale_rows = scale_along(0)

    def grad_state(g, owner, sub, m):
        total = jnp.zeros((HD, HD), F32)
        for i in range(GROUP):
            at = cols(g * GROUP + i)
            scaled = (scale_rows * o[:, at].astype(F32)).astype(BF16)
            s[:, at] = scaled
            total = total + dot(scaled, q[:, at], 0, 0)
        x_out[1, sub, owner, m] = total.astype(BF16)

    for sub in range(SUB):
        loads[2 * sub].wait()
        loads[2 * sub + 1].wait()
        each_group(grad_state, (sub,))

        @pl.when(jnp.logical_not(early))
        def _():
            send_x(x_out, x_in, 0, 1, sub)

    def await_answers(sem, count):
        @pl.when(count > 0)
        def _():
            pl.semaphore_wait(sem, count)

    loads[-2].wait()
    loads[-1].wait()

    def pair_state(g, owner, sub, m):
        x_out[0, sub, owner, m] = dot(k[:, cols(g)], v[:, cols(g)], 0, 0).astype(BF16)

    each_group(pair_state)

    @pl.when(early)
    def _():
        for kind in range(2):
            for sub in range(SUB):
                send_x(x_out, x_in, 0, kind, sub)

    scale_cols = jnp.concatenate([scale_along(1)] * GROUP, axis=1)
    row = lax.broadcasted_iota(jnp.int32, (tokens, tokens), 0)
    col = lax.broadcasted_iota(jnp.int32, (tokens, tokens), 1)
    later = jnp.concatenate([row <= col] * GROUP, axis=1)
    earlier = jnp.concatenate([col <= row] * GROUP, axis=0)

    def within(g):
        key, value = k[:, cols(g)], v[:, cols(g)]
        query, scaled, cot = stacked(q, g), stacked(s, g), stacked(o, g)
        forward = jnp.where(later, scale_cols * dot(key, query, 1, 1), 0.0).astype(BF16)
        backward = jnp.where(later, dot(value, scaled, 1, 1), 0.0).astype(BF16)
        weights = jnp.where(earlier, dot(scaled, value, 1, 1), 0.0).astype(BF16)
        part = dot(weights, key, 1, 0)
        for i in range(GROUP):
            dq_sum[:, cols(g * GROUP + i)] = part[i * tokens : (i + 1) * tokens]
        dk_sum[:, cols(g)] = dot(backward, query, 1, 0)
        dv_sum[:, cols(g)] = dot(forward, cot, 1, 0)

    for g in range(KV):
        within(g)
    @pl.when(jnp.logical_not(early))
    def _():
        for sub in range(SUB):
            send_x(x_out, x_in, 0, 0, sub)

    def each_sub(step, kind):
        for sub in range(SUB):
            step(kind, sub)

    await_answers(here.at[0], ny - 1 - rank)

    @pl.when(early)
    def _():
        each_sub(after_x, 0)
        each_sub(after_x, 1)
        await_answers(here.at[1], nw // 2 - 1 - w)
        each_sub(functools.partial(after_y, end=nw // 2), 0)
        each_sub(after_y, 1)
        each_sub(after_z, 0)
        await_answers(here.at[2], nw // 2)
        for sub in range(SUB):
            start_z(0, sub, nw // 2, nw)
        each_sub(after_yb, 0)
        each_sub(after_z, 1)

    @pl.when(jnp.logical_not(early))
    def _():
        each_sub(after_x, 1)
        each_sub(after_x, 0)
        each_sub(after_y, 1)
        await_answers(here.at[2], nw - 1 - w)
        each_sub(after_y, 0)
        each_sub(after_z, 0)
        each_sub(after_z, 1)
        each_sub(after_yb, 0)

    def finish_query(g, owner, sub, m):
        add = dot(stacked(s, g), state[0, sub, owner, m], 1, 1)
        for i in range(GROUP):
            at = cols(g * GROUP + i)
            dq[:, at] = (dq_sum[:, at] + add[i * tokens : (i + 1) * tokens]).astype(BF16)

    def finish_pair(g, owner, sub, m):
        future = state[1, sub, owner, m]
        at = cols(g)
        dk[:, at] = (dk_sum[:, at] + dot(v[:, at], future, 1, 0)).astype(BF16)
        dv[:, at] = (dv_sum[:, at] + dot(k[:, at], future, 1, 1)).astype(BF16)

    def finish(kind, step):
        for sub in range(SUB):
            all_x(xb_out, state, 3, kind, sub).wait_recv()
            each_group(step, (sub,))

    each_sub(after_yb, 1)
    finish(0, finish_query)
    finish(1, finish_pair)

    for kind in range(2):
        for sub in range(SUB):
            all_x(x_out, x_in, 0, kind, sub).wait_send()
            all_y(y_out, y_in, 1, kind, sub).wait_send()
            all_y(yb_out, yb_in, 2, kind, sub).wait_send()
            all_x(xb_out, state, 3, kind, sub).wait_send()
            low, high = (w + 1, nw) if kind == 0 else (0, w)

            @pl.loop(low, high)
            def _(to):
                z_copy(kind, sub, to, w).wait_send()


def write_back(*refs):
    sources, results, sems = refs[:3], refs[3:6], refs[6]
    copies = [
        pltpu.make_async_copy(source, result, sems.at[i])
        for i, (source, result) in enumerate(zip(sources, results))
    ]
    for copy in copies:
        copy.start()
    for copy in copies:
        copy.wait()


def body(nx, ny, nw, queries, keys, values, out_grad):
    tokens = queries.shape[0]
    mats = KV // nx // SUB
    rows = HD // ny
    wide, narrow = (tokens, queries.shape[1]), (tokens, keys.shape[1])
    by_x = pltpu.VMEM((2, SUB, nx, mats, HD, HD), BF16)
    by_y = pltpu.VMEM((2, SUB, ny, mats, rows, HD), BF16)
    grads = pl.pallas_call(
        functools.partial(kernel, nx, ny, nw),
        out_shape=(
            pltpu.VMEM(wide, BF16),
            pltpu.VMEM(narrow, BF16),
            pltpu.VMEM(narrow, BF16),
        ),
        in_specs=[pl.BlockSpec(memory_space=pltpu.HBM)] * 4,
        out_specs=(pl.BlockSpec(memory_space=pltpu.VMEM),) * 3,
        scratch_shapes=[
            pltpu.VMEM(wide, BF16),
            pltpu.VMEM(narrow, BF16),
            pltpu.VMEM(narrow, BF16),
            pltpu.VMEM(wide, BF16),
            pltpu.VMEM(wide, BF16),
            pltpu.VMEM(wide, F32),
            pltpu.VMEM(narrow, F32),
            pltpu.VMEM(narrow, F32),
            by_x,
            by_x,
            by_y,
            by_y,
            pltpu.VMEM((2, SUB, mats, rows, HD), BF16),
            pltpu.VMEM((2, SUB, nw, mats, rows, HD), BF16),
            by_y,
            by_y,
            by_x,
            by_x,
            pltpu.SemaphoreType.DMA((2 * SUB + 2,)),
            pltpu.SemaphoreType.DMA((4, 2 * SUB)),
            pltpu.SemaphoreType.DMA((4, 2 * SUB)),
            pltpu.SemaphoreType.DMA((SUB, nw)),
            pltpu.SemaphoreType.DMA((SUB, nw)),
            pltpu.SemaphoreType.REGULAR((3,)),
        ],
        compiler_params=pltpu.CompilerParams(
            collective_id=0, has_side_effects=True, vmem_limit_bytes=48 * 2**20
        ),
    )(*(pltpu.with_memory_space_constraint(a, pltpu.HBM) for a in (queries, keys, values, out_grad)))
    return pl.pallas_call(
        write_back,
        out_shape=(pltpu.HBM(wide, BF16), pltpu.HBM(narrow, BF16), pltpu.HBM(narrow, BF16)),
        in_specs=[pl.BlockSpec(memory_space=pltpu.VMEM)] * 3,
        out_specs=(pl.BlockSpec(memory_space=pltpu.HBM),) * 3,
        scratch_shapes=[pltpu.SemaphoreType.DMA((3,))],
        compiler_params=pltpu.CompilerParams(vmem_limit_bytes=16 * 2**20),
    )(*grads)


def solution(mesh, nx=RING_X):
    nw, heads = mesh.shape["seq"], mesh.shape["head"]
    spec = P(("seq", "head"), None)
    return jax.shard_map(
        functools.partial(body, nx, heads // nx, nw),
        mesh=mesh,
        in_specs=(spec,) * 4,
        out_specs=(spec,) * 3,
        check_vma=False,
    )
```

```python
import functools

import jax
import jax.numpy as jnp
from jax import lax
from jax.experimental import pallas as pl
from jax.experimental.pallas import tpu as pltpu
from jax.sharding import PartitionSpec as P

HD = 128
GROUP = 4
KV = 8
RING_X = 4
SUB = 2
MESH = pl.DeviceIdType.MESH
F32 = jnp.float32
BF16 = jnp.bfloat16


def far_first(count):
    return sorted(range(1, count), key=lambda d: -min(d, count - d))


def dot(left, right, left_dim, right_dim):
    return lax.dot_general(
        left, right, (((left_dim,), (right_dim,)), ((), ())), preferred_element_type=F32
    )


def kernel(
    nx, ny, nw,
    q_hbm, k_hbm, v_hbm, o_hbm, dq, dk, dv,
    q, k, v, o, s, dq_sum, dk_sum, dv_sum,
    x_out, x_in, y_out, y_in, z_out, z_in, yb_out, yb_in, xb_out, state,
    load_sem, send_sem, recv_sem, z_send, z_recv, here,
):
    w = lax.axis_index("seq")
    head = lax.axis_index("head")
    y, x = head // nx, head % nx
    mats = KV // nx // SUB
    rows = HD // ny
    tokens = q_hbm.shape[0]

    def half(sub):
        return pl.ds(sub * (q.shape[1] // SUB), q.shape[1] // SUB)

    loads = [
        pltpu.make_async_copy(src, dst, load_sem.at[i])
        for i, (src, dst) in enumerate(
            [
                (ref_from.at[:, half(sub)], ref_to.at[:, half(sub)])
                for sub in range(SUB)
                for ref_from, ref_to in ((o_hbm, o), (q_hbm, q))
            ]
            + [(k_hbm, k), (v_hbm, v)]
        )
    ]
    for load in loads:
        load.start()

    barrier = pltpu.get_barrier_semaphore()

    def greet(seq_to, head_to):
        pl.semaphore_signal(barrier, inc=1, device_id=(seq_to, head_to), device_id_type=MESH)

    for d in far_first(nx):
        greet(w, y * nx + (x + d) % nx)

    def rank_of(place):
        far = 2 * place // (ny + 1)
        return (1 - far) * (2 * place - 1) + far * 2 * (ny - place) + (ny - place) // ny

    rank = rank_of(y)

    def each_column(step, above):
        for d in far_first(ny):
            other = (y + d) % ny

            @pl.when(rank_of(other) > rank if above else rank_of(other) < rank)
            def _():
                step(w, other * nx + x)

    each_column(greet, True)

    @pl.loop(w + 1, nw)
    def _(later_seq):
        greet(later_seq, head)


    first = (w * nx * ny + head) * tokens + 1

    def scale_along(axis):
        place = first + lax.broadcasted_iota(jnp.int32, (tokens, HD), axis)
        return 1.0 / jnp.sqrt((HD * place).astype(F32))

    def chunk(kind, sub):
        return kind * SUB + sub

    def remote(src, dst, stage, c, seq_to, head_to):
        return pltpu.make_async_remote_copy(
            src_ref=src, dst_ref=dst, send_sem=send_sem.at[stage, c], recv_sem=recv_sem.at[stage, c],
            device_id=(seq_to, head_to), device_id_type=MESH,
        )

    def all_x(src, dst, stage, kind, sub):
        return remote(
            src.at[kind, sub, pl.ds(0, nx - 1)], dst.at[kind, sub, pl.ds(0, nx - 1)],
            stage, chunk(kind, sub), w, y * nx + (x + 1) % nx,
        )

    def all_y(src, dst, stage, kind, sub):
        return remote(
            src.at[kind, sub, pl.ds(0, ny - 1)], dst.at[kind, sub, pl.ds(0, ny - 1)],
            stage, chunk(kind, sub), w, (y + 1) % ny * nx + x,
        )

    def send_x(src, dst, stage, kind, sub):
        for d in far_first(nx):
            to = (x + d) % nx
            remote(
                src.at[kind, sub, to], dst.at[kind, sub, x], stage, chunk(kind, sub), w, y * nx + to
            ).start()
        dst[kind, sub, x] = src[kind, sub, x]

    def send_y(src, dst, stage, kind, sub):
        for d in far_first(ny):
            to = (y + d) % ny
            remote(
                src.at[kind, sub, to], dst.at[kind, sub, y], stage, chunk(kind, sub), w, to * nx + x
            ).start()
        dst[kind, sub, y] = src[kind, sub, y]

    def z_copy(kind, sub, to, origin):
        return pltpu.make_async_remote_copy(
            src_ref=z_out.at[kind, sub], dst_ref=z_in.at[kind, sub, origin],
            send_sem=z_send.at[sub, to], recv_sem=z_recv.at[sub, origin],
            device_id=(to, head), device_id_type=MESH,
        )

    def order(kind, count):
        return range(count) if kind == 0 else range(count - 1, -1, -1)

    def after_x(kind, sub):
        all_x(x_out, x_in, 0, kind, sub).wait_recv()
        total = x_in[kind, sub, 0].astype(F32)
        for i in range(1, nx):
            total = total + x_in[kind, sub, i].astype(F32)
        total = total.astype(BF16)
        for i in range(ny):
            y_out[kind, sub, i] = total[:, i * rows : (i + 1) * rows]
        send_y(y_out, y_in, 1, kind, sub)

    def after_y(kind, sub, end=nw):
        all_y(y_out, y_in, 1, kind, sub).wait_recv()
        total = y_in[kind, sub, 0].astype(F32)
        for i in range(1, ny):
            total = total + y_in[kind, sub, i].astype(F32)
        z_out[kind, sub] = total.astype(BF16)
        start_z(kind, sub, *((w + 1, end) if kind == 0 else (0, w)))

    def start_z(kind, sub, low, high):
        @pl.loop(low, high)
        def _(to):
            z_copy(kind, sub, to, w).start()

    def after_z(kind, sub):
        low, high = (0, w) if kind == 0 else (w + 1, nw)

        def add(origin, total):
            z_copy(kind, sub, origin, origin).wait_recv()
            return total + z_in[kind, sub, origin].astype(F32)

        running = lax.fori_loop(low, high, add, jnp.zeros((mats, rows, HD), F32))
        for i in order(kind, ny):
            yb_out[kind, sub, i] = running.astype(BF16)
            running = running + y_in[kind, sub, i].astype(F32)
        send_y(yb_out, yb_in, 2, kind, sub)

    def after_yb(kind, sub):
        all_y(yb_out, yb_in, 2, kind, sub).wait_recv()
        for i in range(ny):
            part = slice(i * rows, (i + 1) * rows)
            running = yb_in[kind, sub, i].astype(F32)
            for j in order(kind, nx):
                xb_out[kind, sub, j, :, part] = running.astype(BF16)
                running = running + x_in[kind, sub, j, :, part].astype(F32)
        send_x(xb_out, state, 3, kind, sub)

    def cols(index):
        return slice(index * HD, (index + 1) * HD)

    def each_group(step, subs=range(SUB)):
        for sub in subs:
            for owner in range(nx):
                for m in range(mats):
                    step(sub * (KV // SUB) + owner * mats + m, owner, sub, m)

    def stacked(ref, g):
        return jnp.concatenate([ref[:, cols(g * GROUP + i)] for i in range(GROUP)], axis=0)

    pl.semaphore_wait(barrier, nx - 1 + rank + w)

    def answer(seq_to, head_to, sem):
        pl.semaphore_signal(sem, inc=1, device_id=(seq_to, head_to), device_id_type=MESH)

    each_column(functools.partial(answer, sem=here.at[0]), False)

    @pl.loop(0, w)
    def _(earlier_seq):
        answer(earlier_seq, head, here.at[1 + w // (nw // 2)])

    early = w < nw // 2

    scale_rows = scale_along(0)

    def grad_state(g, owner, sub, m):
        total = jnp.zeros((HD, HD), F32)
        for i in range(GROUP):
            at = cols(g * GROUP + i)
            scaled = (scale_rows * o[:, at].astype(F32)).astype(BF16)
            s[:, at] = scaled
            total = total + dot(scaled, q[:, at], 0, 0)
        x_out[1, sub, owner, m] = total.astype(BF16)

    for sub in range(SUB):
        loads[2 * sub].wait()
        loads[2 * sub + 1].wait()
        each_group(grad_state, (sub,))

        @pl.when(jnp.logical_not(early))
        def _():
            send_x(x_out, x_in, 0, 1, sub)

    def await_answers(sem, count):
        @pl.when(count > 0)
        def _():
            pl.semaphore_wait(sem, count)

    loads[-2].wait()
    loads[-1].wait()

    def pair_state(g, owner, sub, m):
        x_out[0, sub, owner, m] = dot(k[:, cols(g)], v[:, cols(g)], 0, 0).astype(BF16)

    each_group(pair_state)

    @pl.when(early)
    def _():
        for sub in range(SUB):
            send_x(x_out, x_in, 0, 0, sub)


    scale_cols = jnp.concatenate([scale_along(1)] * GROUP, axis=1)
    row = lax.broadcasted_iota(jnp.int32, (tokens, tokens), 0)
    col = lax.broadcasted_iota(jnp.int32, (tokens, tokens), 1)
    later = jnp.concatenate([row <= col] * GROUP, axis=1)
    earlier = jnp.concatenate([col <= row] * GROUP, axis=0)

    def within(g):
        key, value = k[:, cols(g)], v[:, cols(g)]
        query, scaled, cot = stacked(q, g), stacked(s, g), stacked(o, g)
        forward = jnp.where(later, scale_cols * dot(key, query, 1, 1), 0.0).astype(BF16)
        backward = jnp.where(later, dot(value, scaled, 1, 1), 0.0).astype(BF16)
        weights = jnp.where(earlier, dot(scaled, value, 1, 1), 0.0).astype(BF16)
        part = dot(weights, key, 1, 0)
        for i in range(GROUP):
            dq_sum[:, cols(g * GROUP + i)] = part[i * tokens : (i + 1) * tokens]
        dk_sum[:, cols(g)] = dot(backward, query, 1, 0)
        dv_sum[:, cols(g)] = dot(forward, cot, 1, 0)

    for g in range(KV):
        within(g)

    @pl.when(early)
    def _():
        for sub in range(SUB):
            send_x(x_out, x_in, 0, 1, sub)

    @pl.when(jnp.logical_not(early))
    def _():
        for sub in range(SUB):
            send_x(x_out, x_in, 0, 0, sub)

    def each_sub(step, kind):
        for sub in range(SUB):
            step(kind, sub)

    await_answers(here.at[0], ny - 1 - rank)

    @pl.when(early)
    def _():
        each_sub(after_x, 0)
        each_sub(after_x, 1)
        await_answers(here.at[1], nw // 2 - 1 - w)
        each_sub(functools.partial(after_y, end=nw // 2), 0)
        each_sub(after_y, 1)
        each_sub(after_z, 0)
        await_answers(here.at[2], nw // 2)
        for sub in range(SUB):
            start_z(0, sub, nw // 2, nw)
        each_sub(after_yb, 0)
        each_sub(after_z, 1)

    @pl.when(jnp.logical_not(early))
    def _():
        each_sub(after_x, 1)
        each_sub(after_x, 0)
        each_sub(after_y, 1)
        await_answers(here.at[2], nw - 1 - w)
        each_sub(after_y, 0)
        each_sub(after_z, 0)
        each_sub(after_z, 1)
        each_sub(after_yb, 0)

    def finish_query(g, owner, sub, m):
        add = dot(stacked(s, g), state[0, sub, owner, m], 1, 1)
        for i in range(GROUP):
            at = cols(g * GROUP + i)
            dq[:, at] = (dq_sum[:, at] + add[i * tokens : (i + 1) * tokens]).astype(BF16)

    def finish_pair(g, owner, sub, m):
        future = state[1, sub, owner, m]
        at = cols(g)
        dk[:, at] = (dk_sum[:, at] + dot(v[:, at], future, 1, 0)).astype(BF16)
        dv[:, at] = (dv_sum[:, at] + dot(k[:, at], future, 1, 1)).astype(BF16)

    def finish(kind, step):
        for sub in range(SUB):
            all_x(xb_out, state, 3, kind, sub).wait_recv()
            each_group(step, (sub,))

    each_sub(after_yb, 1)
    finish(0, finish_query)
    for kind in range(2):
        for sub in range(SUB):
            all_x(x_out, x_in, 0, kind, sub).wait_send()
            all_y(y_out, y_in, 1, kind, sub).wait_send()
            all_y(yb_out, yb_in, 2, kind, sub).wait_send()
            low, high = (w + 1, nw) if kind == 0 else (0, w)

            @pl.loop(low, high)
            def _(to):
                z_copy(kind, sub, to, w).wait_send()
    for sub in range(SUB):
        all_x(xb_out, state, 3, 0, sub).wait_send()
    finish(1, finish_pair)
    for sub in range(SUB):
        all_x(xb_out, state, 3, 1, sub).wait_send()


def write_back(*refs):
    sources, results, sems = refs[:3], refs[3:6], refs[6]
    copies = [
        pltpu.make_async_copy(source, result, sems.at[i])
        for i, (source, result) in enumerate(zip(sources, results))
    ]
    for copy in copies:
        copy.start()
    for copy in copies:
        copy.wait()


def body(nx, ny, nw, queries, keys, values, out_grad):
    tokens = queries.shape[0]
    mats = KV // nx // SUB
    rows = HD // ny
    wide, narrow = (tokens, queries.shape[1]), (tokens, keys.shape[1])
    by_x = pltpu.VMEM((2, SUB, nx, mats, HD, HD), BF16)
    by_y = pltpu.VMEM((2, SUB, ny, mats, rows, HD), BF16)
    grads = pl.pallas_call(
        functools.partial(kernel, nx, ny, nw),
        out_shape=(
            pltpu.VMEM(wide, BF16),
            pltpu.VMEM(narrow, BF16),
            pltpu.VMEM(narrow, BF16),
        ),
        in_specs=[pl.BlockSpec(memory_space=pltpu.HBM)] * 4,
        out_specs=(pl.BlockSpec(memory_space=pltpu.VMEM),) * 3,
        scratch_shapes=[
            pltpu.VMEM(wide, BF16),
            pltpu.VMEM(narrow, BF16),
            pltpu.VMEM(narrow, BF16),
            pltpu.VMEM(wide, BF16),
            pltpu.VMEM(wide, BF16),
            pltpu.VMEM(wide, F32),
            pltpu.VMEM(narrow, F32),
            pltpu.VMEM(narrow, F32),
            by_x,
            by_x,
            by_y,
            by_y,
            pltpu.VMEM((2, SUB, mats, rows, HD), BF16),
            pltpu.VMEM((2, SUB, nw, mats, rows, HD), BF16),
            by_y,
            by_y,
            by_x,
            by_x,
            pltpu.SemaphoreType.DMA((2 * SUB + 2,)),
            pltpu.SemaphoreType.DMA((4, 2 * SUB)),
            pltpu.SemaphoreType.DMA((4, 2 * SUB)),
            pltpu.SemaphoreType.DMA((SUB, nw)),
            pltpu.SemaphoreType.DMA((SUB, nw)),
            pltpu.SemaphoreType.REGULAR((3,)),
        ],
        compiler_params=pltpu.CompilerParams(
            collective_id=0, has_side_effects=True, vmem_limit_bytes=48 * 2**20
        ),
    )(*(pltpu.with_memory_space_constraint(a, pltpu.HBM) for a in (queries, keys, values, out_grad)))
    return pl.pallas_call(
        write_back,
        out_shape=(pltpu.HBM(wide, BF16), pltpu.HBM(narrow, BF16), pltpu.HBM(narrow, BF16)),
        in_specs=[pl.BlockSpec(memory_space=pltpu.VMEM)] * 3,
        out_specs=(pl.BlockSpec(memory_space=pltpu.HBM),) * 3,
        scratch_shapes=[pltpu.SemaphoreType.DMA((3,))],
        compiler_params=pltpu.CompilerParams(vmem_limit_bytes=16 * 2**20),
    )(*grads)


def solution(mesh, nx=RING_X):
    nw, heads = mesh.shape["seq"], mesh.shape["head"]
    spec = P(("seq", "head"), None)
    return jax.shard_map(
        functools.partial(body, nx, heads // nx, nw),
        mesh=mesh,
        in_specs=(spec,) * 4,
        out_specs=(spec,) * 3,
        check_vma=False,
    )
```
